32 devices in a mesh: dp: 8 (over z, x), tensor: 4 (over y, core).
Axes of the slice: x: 2, y: 2, z: 4, core: 2. Of those that a mesh axis runs over, the one named last changes fastest.
Arguments:
- hidden_in: bfloat16 [4096, 2048], P(('dp', 'tensor')), may hold values from -6 to 6
- teacher: bfloat16 [4096, 2048], P(('dp', 'tensor')), may hold values from -6 to 6
- cont_lengths: int32 [4, 4], replicated, may hold values from 1 to 128, 384 in all within a row
- query_down: bfloat16 [2048, 1024], P(('dp', 'tensor')), may hold values from -0.125 to 0.125
- key_weight: bfloat16 [2048, 256], P(('dp', 'tensor')), may hold values from -0.125 to 0.125
- value_weight: bfloat16 [2048, 256], P(('dp', 'tensor')), may hold values from -0.125 to 0.125
- attn_gain: bfloat16 [2048], P(('dp', 'tensor')), may hold values from 0.5 to 1.5
- ffn_gain: bfloat16 [2048], P(('dp', 'tensor')), may hold values from 0.5 to 1.5
- query_gain: bfloat16 [1024], P(('dp', 'tensor')), may hold values from 0.5 to 1.5
- query_up: bfloat16 [1024, 4096], P('dp', 'tensor'), may hold values from -0.1875 to 0.1875
- out_weight: bfloat16 [2048, 4096], P('dp', 'tensor'), may hold values from -0.75 to 0.75
- gate_weight: bfloat16 [2048, 5632], P('dp', 'tensor'), may hold values from -0.125 to 0.125
- up_weight: bfloat16 [2048, 5632], P('dp', 'tensor'), may hold values from -0.125 to 0.125
- down_weight: bfloat16 [2048, 5632], P('dp', 'tensor'), may hold values from -0.078125 to 0.078125
Outputs:
- block_out: float32 [4096, 2048], P(('dp', 'tensor'))
- input_grad: float32 [4096, 2048], P(('dp', 'tensor'))
- query_down_grad: float32 [2048, 1024], P(('dp', 'tensor'))
- key_weight_grad: float32 [2048, 256], P(('dp', 'tensor'))
- value_weight_grad: float32 [2048, 256], P(('dp', 'tensor'))
- attn_gain_grad: float32 [2048], P(('dp', 'tensor'))
- ffn_gain_grad: float32 [2048], P(('dp', 'tensor'))
- query_gain_grad: float32 [1024], P(('dp', 'tensor'))
- query_up_grad: float32 [1024, 4096], P('dp', 'tensor')
- out_weight_grad: float32 [2048, 4096], P('dp', 'tensor')
- gate_weight_grad: float32 [2048, 5632], P('dp', 'tensor')
- up_weight_grad: float32 [2048, 5632], P('dp', 'tensor')
- down_weight_grad: float32 [2048, 5632], P('dp', 'tensor')
The draws below stay inside these ranges and needn't reach their ends.
Inputs may be any that keep to these rules, and one draw needn't show every extreme that they name: `cont_lengths`: in each group the 4 continuation lengths sum to 384, and the longest is exactly 128.
All inputs are finite; a program needn't handle non-finite values.
Results may differ from the reference program's by a relative error of at most 0.013.
Values may be sent and summed in bfloat16 or wider, within the bound.
No kernel may reach another device: no remote copies, remote signals or barrier semaphores. Data moves between devices by JAX's collectives and lax.ppermute only.
A program may use at most 256 MiB of HBM per device.

```python
import math
import jax
import jax.numpy as jnp
import numpy as np
from jax import lax

D = 2048
H = 16
HD = 256
QR = 1024
FF = 5632
TOK_DP = 512
CONT = 128
NCONT = 4
GROUPS = 4
TOKENS = 4096


def level_of(stream_key, extent, pieces, least, largest):
    loudness, own = 1.0, jax.random.fold_in(stream_key, 6)
    for position, parts in pieces:
        heights = jnp.exp(jax.random.uniform(jax.random.fold_in(own, position), (parts,), jnp.float32, least / len(pieces), largest / len(pieces)))
        loudness = loudness * jnp.repeat(heights, extent[position] // parts).reshape([-1 if axis == position else 1 for axis in range(len(extent))])
    return loudness


def split_up(amount, total, limit, lean):
    weights = [(1 << 20) // math.isqrt(rank ** lean) + 1 for rank in range(2, amount + 1)]
    rest, counts = total - limit - (amount - 1), [1] * (amount - 1)
    while rest > 0:
        movable = [i for i in range(amount - 1) if counts[i] < limit]
        mass, left = sum([weights[i] for i in movable]), rest
        for i in movable:
            addition = min(limit - counts[i], max(1, left * weights[i] // mass), rest)
            counts[i] = counts[i] + addition
            rest = rest - addition
    return np.array([limit] + counts)


def uneven_parts(stream_key, count, total, most, skew):
    if count == 2:
        one = jax.random.randint(stream_key, (), max(1, total - most), min(most, total - 1) + 1)
        return jnp.stack([one, total - one])
    tallies = jnp.asarray(split_up(count, total, most, skew), jnp.int32)
    pairs = (count - 1) // 2
    giver, sink = tallies[1:1 + 2 * pairs:2], tallies[2:2 + 2 * pairs:2]
    room = jnp.minimum(giver - 1, most - sink)
    moved = jax.random.randint(jax.random.fold_in(stream_key, 1), (pairs,), 0, 1 << 20) % (room + 1)
    tallies = tallies.at[1:1 + 2 * pairs:2].set(giver - moved).at[2:2 + 2 * pairs:2].set(sink + moved)
    return tallies[jax.random.permutation(jax.random.fold_in(stream_key, 2), count)]


def centred(own_key, extent, spread, limit, split=(), kind=jnp.bfloat16):
    result = jax.random.normal(own_key, extent, jnp.float32) * spread
    if len(split) > 0:
        result = level_of(own_key, extent, split, -0.22, 0.18) * result
    return jnp.clip(result, min=-limit, max=limit).astype(kind)


def setup_inputs(seed: int = 0) -> dict:
    keys = jax.random.split(jax.random.key(seed), 15)
    return {
        "hidden_in": centred(keys[0], (TOKENS, D), 1.0, 6.0, ((0, 32),)),
        "teacher": centred(keys[1], (TOKENS, D), 1.0, 6.0, ((0, 32),)),
        "cont_lengths": jax.vmap(lambda own: uneven_parts(own, NCONT, 3 * TOK_DP // 4, CONT, 1))(jax.random.split(keys[2], GROUPS)).reshape((GROUPS, NCONT)).astype(jnp.int32),
        "query_down": centred(keys[3], (D, QR), D ** -0.5, 0.125, ((0, 32),)),
        "key_weight": centred(keys[4], (D, HD), D ** -0.5, 0.125, ((0, 32),)),
        "value_weight": centred(keys[5], (D, HD), D ** -0.5, 0.125, ((0, 32),)),
        "attn_gain": jnp.clip(1.0 + 0.1 * jax.random.normal(keys[6], (D,), jnp.float32), 0.5, 1.5).astype(jnp.bfloat16),
        "ffn_gain": jnp.clip(1.0 + 0.1 * jax.random.normal(keys[7], (D,), jnp.float32), 0.5, 1.5).astype(jnp.bfloat16),
        "query_gain": jnp.clip(1.0 + 0.1 * jax.random.normal(keys[8], (QR,), jnp.float32), 0.5, 1.5).astype(jnp.bfloat16),
        "query_up": centred(keys[9], (QR, H * HD), QR ** -0.5, 0.1875, ((0, 8), (1, 4))),
        "out_weight": centred(keys[10], (D, H * HD), (max(1, H * HD // 64)) ** -0.5, 0.75, ((0, 8), (1, 4))),
        "gate_weight": centred(keys[11], (D, FF), D ** -0.5, 0.125, ((0, 8), (1, 4))),
        "up_weight": centred(keys[12], (D, FF), D ** -0.5, 0.125, ((0, 8), (1, 4))),
        "down_weight": centred(keys[13], (D, FF), FF ** -0.5, 0.078125, ((0, 8), (1, 4))),
    }


EPS = 1e-05
NEG_FILL = -1e+30
ROPE_LOG = math.log(10000.0)

@jax.custom_vjp
def low(v):
    return lax.optimization_barrier(v.astype(jnp.bfloat16)).astype(jnp.float32)

@jax.custom_vjp
def low_back(v):
    return v

def low_keep(v):
    return (low(v), None)

def low_pass(kept, grad):
    return (grad,)

def back_keep(v):
    return (v, None)

def back_low(kept, grad):
    return (low(grad),)
low.defvjp(low_keep, low_pass)
low_back.defvjp(back_keep, back_low)

def matmul(left_op, right_op):
    return jnp.dot(left_op, right_op, precision=lax.Precision.HIGHEST)

def rms(values):
    return values * lax.rsqrt(lax.optimization_barrier(jnp.mean(values * values, axis=-1, keepdims=True)) + EPS)

def rope_tables(positions, head_dim):
    frequency = jnp.exp(jnp.arange(head_dim // 2, dtype=jnp.float32) * (-2.0 * ROPE_LOG / head_dim))
    turned = positions.astype(jnp.float32)[:, None] * frequency[None, :]
    return (jnp.cos(turned), jnp.sin(turned))

def rotate(values, cosine, sine_part):
    middle = values.shape[-1] // 2
    front_part = values[..., :middle]
    back_part = values[..., middle:]
    return jnp.concatenate([front_part * cosine - back_part * sine_part, back_part * cosine + front_part * sine_part], axis=-1)

def row_layout(in_group):
    half_rows = TOK_DP // 2
    half_dev = in_group // TOK_DP
    within = in_group % TOK_DP
    is_prompt = within < half_rows
    prompt_index = half_dev * half_rows + within
    cont_off = jnp.maximum(within - half_rows, 0)
    slot = half_dev * (NCONT // 2) + cont_off // CONT
    inner = cont_off % CONT
    return (is_prompt, prompt_index, slot, inner)

def group_layer(inputs, params):
    latent_proj, key_proj, value_proj, attn_scale, ffn_scale, latent_scale, query_proj, output_proj, gate_proj, lift_proj, drop_proj = params
    rows_all = jnp.arange(2 * TOK_DP, dtype=jnp.int32)
    is_prompt, prompt_index, slot, inner = row_layout(rows_all)
    positions = jnp.where(is_prompt, prompt_index, TOK_DP + inner)
    cosine, sine_part = rope_tables(positions, HD)
    not_prompt = jnp.logical_not(is_prompt)
    prompt_pairs = is_prompt[None, :] & (not_prompt[:, None] | (prompt_index[None, :] <= prompt_index[:, None]))
    cont_pairs = not_prompt[None, :] & not_prompt[:, None] & (slot[None, :] == slot[:, None]) & (inner[None, :] <= inner[:, None])
    allowed = prompt_pairs | cont_pairs
    normed = low(rms(inputs) * attn_scale)
    latent = low_back(matmul(normed, latent_proj))
    latent_normed = low(rms(latent) * latent_scale)
    query_raw = low_back(matmul(latent_normed, query_proj)).reshape(2 * TOK_DP, H, HD)
    queries = low(rotate(query_raw, cosine[:, None, :], sine_part[:, None, :]))
    key_vecs = low(rotate(low_back(matmul(normed, key_proj)), cosine, sine_part))
    value_vecs = low(low_back(matmul(normed, value_proj)))
    scores = low_back(jnp.einsum('qhd,kd->hqk', queries, key_vecs, precision=lax.Precision.HIGHEST) * (1.0 / math.sqrt(HD)))
    scores = jnp.where(allowed[None, :, :], scores, NEG_FILL)
    row_top = lax.optimization_barrier(jnp.max(scores, axis=-1, keepdims=True))
    exp_scores = jnp.exp(scores - row_top)
    attn_probs = low(exp_scores / lax.optimization_barrier(jnp.sum(exp_scores, axis=-1, keepdims=True)))
    mixed_out = low(low_back(jnp.einsum('hqk,kd->qhd', attn_probs, value_vecs, precision=lax.Precision.HIGHEST))).reshape(2 * TOK_DP, H * HD)
    hidden = inputs + low_back(matmul(mixed_out, output_proj.T))
    ffn_in = low(rms(hidden) * ffn_scale)
    gate_pre = low_back(matmul(ffn_in, gate_proj))
    up_pre = low_back(matmul(ffn_in, lift_proj))
    activated = low(jax.nn.silu(gate_pre) * up_pre)
    return hidden + low_back(matmul(activated, drop_proj.T))

def reference(hidden_in, teacher, cont_lengths, query_down, key_weight, value_weight, attn_gain, ffn_gain, query_gain, query_up, out_weight, gate_weight, up_weight, down_weight):
    params = tuple((weight.astype(jnp.float32) for weight in (query_down, key_weight, value_weight, attn_gain, ffn_gain, query_gain, query_up, out_weight, gate_weight, up_weight, down_weight)))
    inputs = hidden_in.astype(jnp.float32).reshape(GROUPS, 2 * TOK_DP, D)
    target = teacher.astype(jnp.float32)
    rows_all = jnp.arange(TOKENS, dtype=jnp.int32)
    in_group = rows_all % (2 * TOK_DP)
    group_of = rows_all // (2 * TOK_DP)
    is_prompt, prompt_index, slot, inner = row_layout(in_group)
    slot_length = cont_lengths[group_of, slot]
    valid_rows = jnp.where(is_prompt, 1.0, jnp.where(inner < slot_length, 1.0, 0.0)).astype(jnp.float32)
    live_count = float(GROUPS * TOK_DP) + jnp.sum(cont_lengths).astype(jnp.float32)
    loss_scale = float(TOKENS) / live_count
    checked = jax.checkpoint(group_layer)

    def objective(layer_in, layer_params):
        outputs = lax.map(lambda group_rows: checked(group_rows, layer_params), layer_in).reshape(TOKENS, D)
        mismatch = outputs - target
        return (0.5 * loss_scale * jnp.sum(valid_rows[:, None] * mismatch * mismatch), outputs)
    loss_value, pullback, block_out = jax.vjp(objective, inputs, params, has_aux=True)
    grad_inputs, grad_params = pullback(jnp.ones_like(loss_value))
    return (block_out, grad_inputs.reshape(TOKENS, D), grad_params[0], grad_params[1], grad_params[2], grad_params[3], grad_params[4], grad_params[5], grad_params[6], grad_params[7], grad_params[8], grad_params[9], grad_params[10])
```

```python
import math

import jax
import jax.numpy as jnp
from jax import lax
from jax.sharding import Mesh
from jax.sharding import PartitionSpec as P

H = 16
HD = 256

EPS = 1e-05
NEG_FILL = -1e30
ROPE_LOG = math.log(10000.0)
BF = jnp.bfloat16
F32 = jnp.float32


SWAP = [(0, 1), (1, 0)]


def inv_rms(values):
    return lax.rsqrt(jnp.mean(values * values, axis=-1, keepdims=True) + EPS)


def norm_back(upstream, values, inverse, gain_vec):
    scaled = upstream * gain_vec
    spread = jnp.mean(scaled * values, axis=-1, keepdims=True)
    result = inverse * scaled - values * (inverse * inverse * inverse) * spread
    return (result, jnp.sum(upstream * values * inverse, axis=0))


def rope_tables(positions, head_dim):
    frequency = jnp.exp(jnp.arange(head_dim // 2, dtype=F32) * (-2.0 * ROPE_LOG / head_dim))
    turned = positions.astype(F32)[:, None] * frequency[None, :]
    return (jnp.cos(turned), jnp.sin(turned))


def rotate(values, cosine, sine_part):
    middle = values.shape[-1] // 2
    front_part = values[..., :middle]
    back_part = values[..., middle:]
    return jnp.concatenate(
        [front_part * cosine - back_part * sine_part, back_part * cosine + front_part * sine_part],
        axis=-1,
    )


def contract(left_op, right_op, left_dim, right_dim):
    return lax.dot_general(
        left_op,
        right_op,
        (((left_dim,), (right_dim,)), ((), ())),
        preferred_element_type=F32,
    )


def to_h(value):
    return lax.ppermute(value, "h", SWAP)


def to_a(value):
    return lax.ppermute(value, "a", SWAP)


def to_ha(value):
    return lax.ppermute(value, ("h", "a"), [(i, 3 - i) for i in range(4)])


def to_c(value):
    return lax.ppermute(value, "c", SWAP)


def plane_gather(block):
    near = jnp.concatenate([block, to_a(block), to_h(block), to_ha(block)], axis=0)
    return near, to_c(near)


def plane_scatter(near, far):
    joined = lax.optimization_barrier(near.astype(BF)).astype(F32) + to_c(far.astype(BF)).astype(F32)
    rows = joined.shape[0] // 4
    pieces = [joined[i * rows : (i + 1) * rows] for i in range(4)]
    return (
        pieces[0]
        + to_a(pieces[1].astype(BF)).astype(F32)
        + to_h(pieces[2].astype(BF)).astype(F32)
        + to_ha(pieces[3].astype(BF)).astype(F32)
    )


def flip_if(bit, value, axis):
    first = lax.slice_in_dim(value, 0, 1, axis=axis)
    second = lax.slice_in_dim(value, 1, 2, axis=axis)
    return jnp.concatenate(
        [jnp.where(bit, second, first), jnp.where(bit, first, second)], axis=axis
    )


def g_size():
    return lax.axis_size("g")


def g_flip(value, axis):
    if g_size() != 4:
        return value
    place = lax.axis_index("g")
    shape = value.shape
    split = shape[:axis] + (2, 2, shape[axis] // 4) + shape[axis + 1 :]
    value = value.reshape(split)
    value = flip_if(place // 2 == 1, value, axis)
    value = flip_if(place % 2 == 1, value, axis + 1)
    return value.reshape(shape)


def g_gather(block):
    count = g_size()
    if count != 4:
        whole = lax.all_gather(block, "g", axis=0, tiled=True)
        rows = block.shape[0]
        return [whole[i * rows : (i + 1) * rows] for i in range(count)]
    two = lax.ppermute(block, "g", [(i, i ^ 2) for i in range(4)])
    middle = lax.ppermute(block, "g", [(1, 2), (2, 1)])
    one = lax.ppermute(block, "g", [(i, i ^ 1) for i in range(4)])
    outer = lax.ppermute(two, "g", [(2, 3), (1, 0)])
    place = lax.axis_index("g")
    three = jnp.where((place == 1) | (place == 2), middle, outer)
    return [block, one, two, three]


def g_scatter(blocks):
    if g_size() != 4:
        whole = jnp.concatenate(blocks, axis=0)
        return lax.psum_scatter(whole, "g", scatter_dimension=0, tiled=True).astype(F32)
    relay = lax.ppermute(blocks[3], "g", [(0, 1), (3, 2)])
    middle = lax.ppermute(blocks[3], "g", [(1, 2), (2, 1)])
    one = lax.ppermute(blocks[1], "g", [(i, i ^ 1) for i in range(4)])
    longer = (blocks[2].astype(F32) + relay.astype(F32)).astype(BF)
    two = lax.ppermute(longer, "g", [(i, i ^ 2) for i in range(4)])
    return (
        blocks[0].astype(F32) + one.astype(F32) + middle.astype(F32) + two.astype(F32)
    )


def local(
    hidden_in,
    teacher,
    cont_lengths,
    query_down,
    key_weight,
    value_weight,
    attn_gain,
    ffn_gain,
    query_gain,
    query_up,
    out_weight,
    gate_weight,
    up_weight,
    down_weight,
):
    groups = g_size()
    g_place = lax.axis_index("g")
    h_place = lax.axis_index("h")
    a_place = lax.axis_index("a")
    c_place = lax.axis_index("c")
    is_first = h_place == 0
    rows = hidden_in.shape[0]
    width = hidden_in.shape[1]
    plane = 2 * lax.axis_size("a") * lax.axis_size("c")
    w_rows = query_down.shape[0]
    rank = query_down.shape[1]
    q_rows = query_gain.shape[0]
    slice_rows = groups * w_rows
    pack_cols = rank + 2 * HD
    heads_local = H // plane
    score_scale = 1.0 / math.sqrt(HD)

    def plane_order(value):
        value = flip_if(h_place == 1, value, 0)
        value = flip_if(a_place == 1, value, 1)
        value = flip_if(c_place == 1, value, 2)
        return jnp.moveaxis(value, 2, 0)

    def plane_back(value):
        value = flip_if(c_place == 1, value, 0)
        value = flip_if(h_place == 1, value, 1)
        value = flip_if(a_place == 1, value, 2)
        return jnp.moveaxis(value, 0, 2)

    def halves_swapped(weights):
        own, sent = [], []
        for weight in weights:
            half = weight.shape[1] // 2
            left, right = weight[:, :half], weight[:, half:]
            own.append(jnp.where(is_first, left, right))
            sent.append(jnp.where(is_first, right, left))
        came = to_h(jnp.concatenate(sent, axis=0))
        pieces = []
        begin = 0
        for kept in own:
            other = came[begin : begin + kept.shape[0]]
            begin = begin + kept.shape[0]
            pieces.append(jnp.where(is_first, kept, other))
            pieces.append(jnp.where(is_first, other, kept))
        return jnp.concatenate(pieces, axis=0)

    def gathered(weights):
        blocks = g_gather(halves_swapped(weights))
        results = []
        begin = 0
        for weight in weights:
            size = 2 * weight.shape[0]
            results.append(
                jnp.concatenate([block[begin : begin + size] for block in blocks], axis=0)
            )
            begin = begin + size
        return results

    gain_cols = jnp.stack(
        [attn_gain, ffn_gain, jnp.pad(query_gain, (0, w_rows - q_rows))], axis=1
    )
    shared = jnp.concatenate(
        [query_down, key_weight, value_weight, jnp.pad(gain_cols, ((0, 0), (0, 125)))], axis=1
    )
    shared_slice = jnp.concatenate(g_gather(shared), axis=0)
    shared_proj = shared_slice[:, :pack_cols]
    query_proj, output_proj = gathered([query_up, out_weight])
    gate_proj, lift_proj = gathered([gate_weight, up_weight])
    (drop_proj,) = gathered([down_weight])

    own_gains = shared_slice[:, pack_cols : pack_cols + 3].T
    near_gains, far_gains = plane_gather(jnp.pad(own_gains, ((0, 13), (0, 0))))
    all_gains = jnp.concatenate([near_gains, far_gains], axis=0).reshape(
        2, 2, 2, 16, slice_rows
    )[:, :, :, :3]
    all_gains = plane_back(all_gains).reshape(plane, 3, groups, w_rows).astype(F32)
    all_gains = jnp.transpose(all_gains, (1, 2, 0, 3))
    attn_scale = all_gains[0].reshape(width)
    ffn_scale = all_gains[1].reshape(width)
    latent_scale = all_gains[2, :, :, :q_rows].reshape(rank)

    order = jnp.arange(plane, dtype=jnp.int32)
    block_c = c_place ^ (order // 4)
    block_h = h_place ^ (order // 2 % 2)
    block_a = a_place ^ (order % 2)
    block_unit = block_h * 2 + block_c
    within = jnp.arange(rows, dtype=jnp.int32)
    prompt_total = 4 * rows
    positions = jnp.where(
        block_a[:, None] == 0, block_unit[:, None] * rows + within[None, :], prompt_total + within
    ).reshape(plane * rows)
    row_prompt = jnp.repeat(block_a == 0, rows)
    row_unit = jnp.repeat(block_unit, rows)
    cosine, sine_part = rope_tables(positions, HD)
    half_count = 4 * rows

    inputs = g_flip(hidden_in, 1).astype(F32)
    first_inv = inv_rms(inputs)
    normed = (inputs * first_inv * attn_scale).astype(BF)
    slices = normed.reshape(rows, groups, plane, w_rows).transpose(2, 0, 1, 3)
    slices = plane_order(slices.reshape(2, 2, 2, rows, slice_rows)).reshape(
        2, 4, rows, slice_rows
    )
    near_slices = slices[0]
    far_slices = to_c(slices[1])
    from_a = to_a(jnp.stack([near_slices[1], far_slices[1]]))
    from_h = to_h(jnp.stack([near_slices[2], far_slices[2]]))
    from_ha = to_ha(jnp.stack([near_slices[3], far_slices[3]]))
    normed_near = jnp.stack([near_slices[0], from_a[0], from_h[0], from_ha[0]])
    normed_far = jnp.stack([far_slices[0], from_a[1], from_h[1], from_ha[1]])
    flat = (half_count, slice_rows)
    packed = plane_scatter(
        jnp.dot(normed_near.reshape(flat), shared_proj, preferred_element_type=F32),
        jnp.dot(normed_far.reshape(flat), shared_proj, preferred_element_type=F32),
    )
    latent = g_flip(packed[:, :rank], 1)
    latent_inv = inv_rms(latent)
    latent_normed = (latent * latent_inv * latent_scale).astype(BF)
    own_cosine, own_sine = cosine[:rows], sine_part[:rows]
    own_keys = rotate(packed[:, rank : rank + HD], own_cosine, own_sine).astype(BF)
    own_values = packed[:, rank + HD :].astype(BF)
    pack_halves = plane_gather(jnp.concatenate([latent_normed, own_keys, own_values], axis=1))
    latent_halves = [half[:, :rank] for half in pack_halves]
    key_all = jnp.concatenate([half[:, rank : rank + HD] for half in pack_halves], axis=0)
    value_all = jnp.concatenate([half[:, rank + HD :] for half in pack_halves], axis=0)

    def rows_of(index):
        return slice(index * half_count, (index + 1) * half_count)

    query_halves = []
    for index in range(2):
        raw = jnp.dot(latent_halves[index], query_proj, preferred_element_type=F32)
        raw = raw.reshape(half_count, heads_local, HD)
        query_halves.append(
            rotate(
                raw, cosine[rows_of(index), None, :], sine_part[rows_of(index), None, :]
            ).astype(BF)
        )
    queries = jnp.concatenate(query_halves, axis=0)
    in_order = positions[None, :] <= positions[:, None]
    allowed = (
        row_prompt[None, :] & (jnp.logical_not(row_prompt)[:, None] | in_order)
    ) | (
        jnp.logical_not(row_prompt)[None, :]
        & jnp.logical_not(row_prompt)[:, None]
        & (row_unit[None, :] == row_unit[:, None])
        & in_order
    )

    def all_scores():
        scores = (
            jnp.einsum("qhd,kd->hqk", queries, key_all, preferred_element_type=F32) * score_scale
        )
        return jnp.where(allowed[None, :, :], scores, NEG_FILL)

    scores = all_scores()
    row_top = jnp.max(scores, axis=-1, keepdims=True)
    exp_scores = jnp.exp(scores - row_top)
    row_total = jnp.sum(exp_scores, axis=-1, keepdims=True)
    attn_probs = (exp_scores / row_total).astype(BF)
    lse = row_top + jnp.log(row_total)
    mixed = (
        jnp.einsum("hqk,kd->qhd", attn_probs, value_all, preferred_element_type=F32)
        .astype(BF)
        .reshape(plane * rows, heads_local * HD)
    )
    mixed_halves = [mixed[rows_of(0)], mixed[rows_of(1)]]
    attn_total = plane_scatter(*[contract(half, output_proj, 1, 1) for half in mixed_halves])
    hidden = inputs + attn_total

    second_inv = inv_rms(hidden)
    ffn_in = (hidden * second_inv * ffn_scale).astype(BF)
    ffn_halves = plane_gather(ffn_in)
    gate_pre = [jnp.dot(half, gate_proj, preferred_element_type=F32) for half in ffn_halves]
    up_pre = [jnp.dot(half, lift_proj, preferred_element_type=F32) for half in ffn_halves]
    activated = [
        (jax.nn.silu(gate) * lift).astype(BF) for gate, lift in zip(gate_pre, up_pre)
    ]
    ffn_total = plane_scatter(*[contract(half, drop_proj, 1, 1) for half in activated])
    block_out = hidden + ffn_total

    group_total = cont_lengths.shape[0]
    slot_total = cont_lengths.shape[1]
    pick_group = jnp.arange(group_total, dtype=jnp.int32) == g_place
    pick_slot = jnp.arange(slot_total, dtype=jnp.int32) == h_place * 2 + c_place
    own_length = jnp.sum(
        jnp.where(pick_group[:, None] & pick_slot[None, :], cont_lengths, 0)
    )
    valid_rows = jnp.logical_or(a_place == 0, within < own_length).astype(F32)
    live_count = float(group_total * prompt_total) + jnp.sum(cont_lengths).astype(F32)
    loss_scale = float(groups * plane * rows) / live_count
    target = g_flip(teacher, 1).astype(F32)
    out_grad = loss_scale * valid_rows[:, None] * (block_out - target)

    out_halves = plane_gather(out_grad.astype(BF))
    grad_gate = []
    grad_lift = []
    for index in range(2):
        grad_act = jnp.dot(out_halves[index], drop_proj, preferred_element_type=F32)
        gate = gate_pre[index]
        sigmoid_gate = jax.nn.sigmoid(gate)
        grad_gate.append(
            (grad_act * up_pre[index] * sigmoid_gate * (1.0 + gate * (1.0 - sigmoid_gate))).astype(
                BF
            )
        )
        grad_lift.append((grad_act * gate * sigmoid_gate).astype(BF))

    def row_product(left, right):
        return sum(contract(one, two, 0, 0) for one, two in zip(left, right)).astype(BF)

    def reduced(grads):
        blocks = []
        for index in range(groups):
            pieces = []
            for grad in grads:
                size = grad.shape[0] // groups
                pieces.append(grad[index * size : (index + 1) * size])
            blocks.append(jnp.concatenate(pieces, axis=0))
        total = g_scatter(blocks)
        kept, sent = [], []
        begin = 0
        for grad in grads:
            size = grad.shape[0] // groups // 2
            top = total[begin : begin + size]
            low = total[begin + size : begin + 2 * size]
            begin = begin + 2 * size
            kept.append(jnp.where(is_first, top, low))
            sent.append(jnp.where(is_first, low, top))
        came = to_h(jnp.concatenate(sent, axis=0).astype(BF)).astype(F32)
        results = []
        begin = 0
        for own in kept:
            other = came[begin : begin + own.shape[0]]
            begin = begin + own.shape[0]
            results.append(
                jnp.concatenate(
                    [jnp.where(is_first, own, other), jnp.where(is_first, other, own)], axis=1
                )
            )
        return results

    (drop_sum,) = reduced([row_product(out_halves, activated)])
    gate_sum, lift_sum = reduced(
        [row_product(ffn_halves, grad_gate), row_product(ffn_halves, grad_lift)]
    )
    grad_ffn_in = plane_scatter(
        *[
            contract(grad_gate[index], gate_proj, 1, 1)
            + contract(grad_lift[index], lift_proj, 1, 1)
            for index in range(2)
        ]
    )
    ffn_back, ffn_gain_part = norm_back(grad_ffn_in, hidden, second_inv, ffn_scale)
    grad_hidden = out_grad + ffn_back

    branch_halves = plane_gather(grad_hidden.astype(BF))
    grad_mixed = jnp.concatenate(
        [
            jnp.dot(half, output_proj, preferred_element_type=F32).astype(BF)
            for half in branch_halves
        ],
        axis=0,
    ).reshape(plane * rows, heads_local, HD)
    output_grad = row_product(branch_halves, mixed_halves)
    probs = jnp.exp(all_scores() - lse)
    grad_probs = jnp.einsum("qhd,kd->hqk", grad_mixed, value_all, preferred_element_type=F32)
    center = jnp.sum(probs * grad_probs, axis=-1, keepdims=True)
    grad_scores = (probs * (grad_probs - center)).astype(BF)
    grad_query = (
        jnp.einsum("hqk,kd->qhd", grad_scores, key_all, preferred_element_type=F32) * score_scale
    )
    key_grad = (
        jnp.einsum("hqk,qhd->kd", grad_scores, queries, preferred_element_type=F32) * score_scale
    )
    value_grad = jnp.einsum(
        "hqk,qhd->kd", probs.astype(BF), grad_mixed, preferred_element_type=F32
    )
    grad_query_raw = (
        rotate(grad_query, cosine[:, None, :], -sine_part[:, None, :])
        .reshape(plane * rows, heads_local * HD)
        .astype(BF)
    )
    raw_halves = [grad_query_raw[rows_of(0)], grad_query_raw[rows_of(1)]]
    query_up_grad = row_product(latent_halves, raw_halves)
    query_up_sum, output_sum = reduced([query_up_grad, output_grad])
    pair_total = plane_scatter(
        *[
            jnp.concatenate(
                [
                    contract(raw_halves[index], query_proj, 1, 1),
                    key_grad[rows_of(index)],
                    value_grad[rows_of(index)],
                ],
                axis=1,
            )
            for index in range(2)
        ]
    )
    latent_back, query_gain_part = norm_back(
        pair_total[:, :rank], latent, latent_inv, latent_scale
    )
    grad_key_raw = rotate(pair_total[:, rank : rank + HD], own_cosine, -own_sine)
    grad_pack = jnp.concatenate(
        [g_flip(latent_back, 1), grad_key_raw, pair_total[:, rank + HD :]], axis=1
    ).astype(BF)
    gain_rows = jnp.concatenate([query_gain_part, ffn_gain_part]).reshape(2, pack_cols)
    padded = rows + 16
    grad_pack = jnp.concatenate(
        [grad_pack, jnp.pad(gain_rows, ((0, 14), (0, 0))).astype(BF)], axis=0
    )
    pack_grads = plane_gather(grad_pack)
    wide_normed = [
        jnp.pad(half, ((0, 0), (0, 16), (0, 0))).reshape(4 * padded, slice_rows)
        for half in (normed_near, normed_far)
    ]
    shared_grad = sum(contract(one, two, 0, 0) for one, two in zip(wide_normed, pack_grads))
    slice_grads = [contract(half, shared_proj, 1, 1) for half in pack_grads]
    attn_gain_slice = sum(
        jnp.sum(grad * value.astype(F32), axis=0)
        for grad, value in zip(slice_grads, wide_normed)
    ) / shared_slice[:, pack_cols].astype(F32)
    gain_totals = sum(
        jnp.sum(half.reshape(4, padded, pack_cols)[:, rows : rows + 2].astype(F32), axis=0)
        for half in pack_grads
    ).reshape(rank + width)
    place = h_place * 4 + a_place * 2 + c_place
    query_gain_slice = lax.dynamic_index_in_dim(
        gain_totals[:rank].reshape(groups, plane, q_rows), place, 1, keepdims=False
    )
    query_gain_slice = jnp.pad(query_gain_slice, ((0, 0), (0, w_rows - q_rows)))
    ffn_gain_slice = lax.dynamic_index_in_dim(
        gain_totals[rank:].reshape(groups, plane, w_rows), place, 1, keepdims=False
    )
    gain_grad_cols = jnp.stack(
        [attn_gain_slice, ffn_gain_slice.reshape(slice_rows), query_gain_slice.reshape(slice_rows)],
        axis=1,
    )
    shared_out = jnp.concatenate(
        [shared_grad, jnp.pad(gain_grad_cols, ((0, 0), (0, 125)))], axis=1
    ).astype(BF)
    shared_sum = g_scatter(
        [shared_out[index * w_rows : (index + 1) * w_rows] for index in range(groups)]
    )

    near_grad, far_grad = [
        grad.reshape(4, padded, slice_rows)[:, :rows].astype(BF) for grad in slice_grads
    ]
    back_a = to_a(jnp.stack([near_grad[1], far_grad[1]]))
    back_h = to_h(jnp.stack([near_grad[2], far_grad[2]]))
    back_ha = to_ha(jnp.stack([near_grad[3], far_grad[3]]))
    mine = jnp.stack([near_grad[0], back_a[0], back_h[0], back_ha[0]])
    others = to_c(jnp.stack([far_grad[0], back_a[1], back_h[1], back_ha[1]]))
    grad_normed = plane_back(
        jnp.stack([mine, others]).reshape(2, 2, 2, rows, slice_rows)
    ).reshape(plane, rows, groups, w_rows)
    grad_normed = grad_normed.transpose(1, 2, 0, 3).reshape(rows, width).astype(F32)
    first_back, _ = norm_back(grad_normed, inputs, first_inv, attn_scale)
    input_grad = grad_hidden + first_back

    return (
        g_flip(block_out, 1),
        g_flip(input_grad, 1),
        shared_sum[:, :rank],
        shared_sum[:, rank : rank + HD],
        shared_sum[:, rank + HD : pack_cols],
        shared_sum[:, pack_cols],
        shared_sum[:, pack_cols + 1],
        shared_sum[:q_rows, pack_cols + 2],
        query_up_sum,
        output_sum,
        gate_sum,
        lift_sum,
        drop_sum,
    )


def solution(mesh):
    dp, tensor = mesh.shape["dp"], mesh.shape["tensor"]
    fine = Mesh(mesh.devices.reshape(dp // 2, 2, tensor // 2, 2), ("g", "h", "a", "c"))
    rows = P(("g", "h", "a", "c"), None)
    vector = P(("g", "h", "a", "c"))
    block = P(("g", "h"), ("a", "c"))
    return jax.shard_map(
        local,
        mesh=fine,
        in_specs=(rows, rows, P()) + (rows,) * 3 + (vector,) * 3 + (block,) * 5,
        out_specs=(rows,) * 5 + (vector,) * 3 + (block,) * 5,
        check_vma=False,
    )
```

```python
import math

import jax
import jax.numpy as jnp
from jax import lax
from jax.sharding import Mesh
from jax.sharding import PartitionSpec as P


H = 16
HD = 256

EPS = 1e-05
NEG_FILL = -1e30
ROPE_LOG = math.log(10000.0)
BF = jnp.bfloat16
F32 = jnp.float32


SWAP = [(0, 1), (1, 0)]


def inv_rms(values):
    return lax.rsqrt(jnp.mean(values * values, axis=-1, keepdims=True) + EPS)


def norm_back(upstream, values, inverse, gain_vec):
    scaled = upstream * gain_vec
    spread = jnp.mean(scaled * values, axis=-1, keepdims=True)
    result = inverse * scaled - values * (inverse * inverse * inverse) * spread
    return (result, jnp.sum(upstream * values * inverse, axis=0))


def rope_tables(positions, head_dim):
    frequency = jnp.exp(jnp.arange(head_dim // 2, dtype=F32) * (-2.0 * ROPE_LOG / head_dim))
    turned = positions.astype(F32)[:, None] * frequency[None, :]
    return (jnp.cos(turned), jnp.sin(turned))


def rotate(values, cosine, sine_part):
    middle = values.shape[-1] // 2
    front_part = values[..., :middle]
    back_part = values[..., middle:]
    return jnp.concatenate(
        [front_part * cosine - back_part * sine_part, back_part * cosine + front_part * sine_part],
        axis=-1,
    )


def contract(left_op, right_op, left_dim, right_dim):
    return lax.dot_general(
        left_op,
        right_op,
        (((left_dim,), (right_dim,)), ((), ())),
        preferred_element_type=F32,
    )


def to_h(value):
    return lax.ppermute(value, "h", SWAP)


def to_a(value):
    return lax.ppermute(value, "a", SWAP)


def to_ha(value):
    return lax.ppermute(value, ("h", "a"), [(i, 3 - i) for i in range(4)])


def to_c(value):
    return lax.ppermute(value, "c", SWAP)


def plane_gather(block):
    near = jnp.concatenate([block, to_a(block), to_h(block), to_ha(block)], axis=0)
    return near, to_c(near)


def plane_scatter(near, far):
    joined = lax.optimization_barrier(near.astype(BF)).astype(F32)
    joined = joined + to_c(far.astype(BF)).astype(F32)
    rows = joined.shape[0] // 4
    pieces = [joined[i * rows : (i + 1) * rows] for i in range(4)]
    return (
        pieces[0]
        + to_a(pieces[1].astype(BF)).astype(F32)
        + to_h(pieces[2].astype(BF)).astype(F32)
        + to_ha(pieces[3].astype(BF)).astype(F32)
    )


def flip_if(bit, value, axis):
    first = lax.slice_in_dim(value, 0, 1, axis=axis)
    second = lax.slice_in_dim(value, 1, 2, axis=axis)
    return jnp.concatenate(
        [jnp.where(bit, second, first), jnp.where(bit, first, second)], axis=axis
    )


def g_size():
    return lax.axis_size("g")


def g_flip(value, axis):
    if g_size() != 4:
        return value
    place = lax.axis_index("g")
    shape = value.shape
    split = shape[:axis] + (2, 2, shape[axis] // 4) + shape[axis + 1 :]
    value = value.reshape(split)
    value = flip_if(place // 2 == 1, value, axis)
    value = flip_if(place % 2 == 1, value, axis + 1)
    return value.reshape(shape)


def g_gather(block):
    count = g_size()
    if count != 4:
        whole = lax.all_gather(block, "g", axis=0, tiled=True)
        rows = block.shape[0]
        return [whole[i * rows : (i + 1) * rows] for i in range(count)]
    two = lax.ppermute(block, "g", [(i, i ^ 2) for i in range(4)])
    middle = lax.ppermute(block, "g", [(1, 2), (2, 1)])
    one = lax.ppermute(block, "g", [(i, i ^ 1) for i in range(4)])
    outer = lax.ppermute(two, "g", [(2, 3), (1, 0)])
    place = lax.axis_index("g")
    three = jnp.where((place == 1) | (place == 2), middle, outer)
    return [block, one, two, three]


def g_scatter(blocks):
    if g_size() != 4:
        whole = jnp.concatenate(blocks, axis=0)
        return [lax.psum_scatter(whole, "g", scatter_dimension=0, tiled=True)]
    relay = lax.ppermute(blocks[3], "g", [(0, 1), (3, 2)])
    middle = lax.ppermute(blocks[3], "g", [(1, 2), (2, 1)])
    one = lax.ppermute(blocks[1], "g", [(i, i ^ 1) for i in range(4)])
    longer = (blocks[2].astype(F32) + relay.astype(F32)).astype(BF)
    two = lax.ppermute(longer, "g", [(i, i ^ 2) for i in range(4)])
    return [blocks[0], one, middle, two]


def g_sum(terms, later):
    terms, _ = lax.optimization_barrier((terms, later))
    return sum(term.astype(F32) for term in terms)


def layer(
    hidden_in,
    teacher,
    cont_lengths,
    query_down,
    key_weight,
    value_weight,
    attn_gain,
    ffn_gain,
    query_gain,
    query_up,
    out_weight,
    gate_weight,
    up_weight,
    down_weight,
):
    groups = g_size()
    g_place = lax.axis_index("g")
    h_place = lax.axis_index("h")
    a_place = lax.axis_index("a")
    c_place = lax.axis_index("c")
    is_first = h_place == 0
    rows = hidden_in.shape[0]
    width = hidden_in.shape[1]
    plane = 2 * lax.axis_size("a") * lax.axis_size("c")
    w_rows = query_down.shape[0]
    rank = query_down.shape[1]
    q_rows = query_gain.shape[0]
    slice_rows = groups * w_rows
    pack_cols = rank + 2 * HD
    heads_local = H // plane
    score_scale = 1.0 / math.sqrt(HD)

    def plane_order(value):
        value = flip_if(h_place == 1, value, 0)
        value = flip_if(a_place == 1, value, 1)
        value = flip_if(c_place == 1, value, 2)
        return jnp.moveaxis(value, 2, 0)

    def plane_back(value):
        value = flip_if(c_place == 1, value, 0)
        value = flip_if(h_place == 1, value, 1)
        value = flip_if(a_place == 1, value, 2)
        return jnp.moveaxis(value, 0, 2)

    def halves_swapped(weights):
        own, sent = [], []
        for weight in weights:
            half = weight.shape[1] // 2
            left, right = weight[:, :half], weight[:, half:]
            own.append(jnp.where(is_first, left, right))
            sent.append(jnp.where(is_first, right, left))
        came = to_h(jnp.concatenate(sent, axis=0))
        pieces = []
        begin = 0
        for kept in own:
            other = came[begin : begin + kept.shape[0]]
            begin = begin + kept.shape[0]
            pieces.append(jnp.where(is_first, kept, other))
            pieces.append(jnp.where(is_first, other, kept))
        return jnp.concatenate(pieces, axis=0)

    def gathered(weights):
        blocks = g_gather(halves_swapped(weights))
        results = []
        begin = 0
        for weight in weights:
            size = 2 * weight.shape[0]
            results.append(
                jnp.concatenate([block[begin : begin + size] for block in blocks], axis=0)
            )
            begin = begin + size
        return results

    gain_cols = jnp.stack(
        [attn_gain, ffn_gain, jnp.pad(query_gain, (0, w_rows - q_rows))], axis=1
    )
    shared = jnp.concatenate(
        [query_down, key_weight, value_weight, jnp.pad(gain_cols, ((0, 0), (0, 125)))], axis=1
    )
    shared_slice = jnp.concatenate(g_gather(shared), axis=0)
    shared_proj = shared_slice[:, :pack_cols]
    query_proj, output_proj = gathered([query_up, out_weight])
    gate_proj, lift_proj = gathered([gate_weight, up_weight])
    (drop_proj,) = gathered([down_weight])

    own_gains = shared_slice[:, pack_cols : pack_cols + 3].T
    near_gains, far_gains = plane_gather(jnp.pad(own_gains, ((0, 13), (0, 0))))
    all_gains = jnp.concatenate([near_gains, far_gains], axis=0).reshape(
        2, 2, 2, 16, slice_rows
    )[:, :, :, :3]
    all_gains = plane_back(all_gains).reshape(plane, 3, groups, w_rows).astype(F32)
    all_gains = jnp.transpose(all_gains, (1, 2, 0, 3))
    attn_scale = all_gains[0].reshape(width)
    ffn_scale = all_gains[1].reshape(width)
    latent_scale = all_gains[2, :, :, :q_rows].reshape(rank)

    order = jnp.arange(plane, dtype=jnp.int32)
    block_c = c_place ^ (order // 4)
    block_h = h_place ^ (order // 2 % 2)
    block_a = a_place ^ (order % 2)
    block_unit = block_h * 2 + block_c
    within = jnp.arange(rows, dtype=jnp.int32)
    prompt_total = 4 * rows
    positions = jnp.where(
        block_a[:, None] == 0, block_unit[:, None] * rows + within[None, :], prompt_total + within
    ).reshape(plane * rows)
    row_prompt = jnp.repeat(block_a == 0, rows)
    row_unit = jnp.repeat(block_unit, rows)
    cosine, sine_part = rope_tables(positions, HD)
    half_count = 4 * rows

    inputs = g_flip(hidden_in, 1).astype(F32)
    first_inv = inv_rms(inputs)
    normed = (inputs * first_inv * attn_scale).astype(BF)
    slices = normed.reshape(rows, groups, plane, w_rows).transpose(2, 0, 1, 3)
    slices = plane_order(slices.reshape(2, 2, 2, rows, slice_rows)).reshape(
        2, 4, rows, slice_rows
    )
    near_slices = slices[0]
    far_slices = to_c(slices[1])
    from_a = to_a(jnp.stack([near_slices[1], far_slices[1]]))
    from_h = to_h(jnp.stack([near_slices[2], far_slices[2]]))
    from_ha = to_ha(jnp.stack([near_slices[3], far_slices[3]]))
    normed_near = jnp.stack([near_slices[0], from_a[0], from_h[0], from_ha[0]])
    normed_far = jnp.stack([far_slices[0], from_a[1], from_h[1], from_ha[1]])
    flat = (half_count, slice_rows)
    packed = plane_scatter(
        jnp.dot(normed_near.reshape(flat), shared_proj, preferred_element_type=F32),
        jnp.dot(normed_far.reshape(flat), shared_proj, preferred_element_type=F32),
    )
    latent = g_flip(packed[:, :rank], 1)
    latent_inv = inv_rms(latent)
    latent_normed = (latent * latent_inv * latent_scale).astype(BF)
    own_cosine, own_sine = cosine[:rows], sine_part[:rows]
    own_keys = rotate(packed[:, rank : rank + HD], own_cosine, own_sine).astype(BF)
    own_values = packed[:, rank + HD :].astype(BF)
    pack_halves = plane_gather(jnp.concatenate([latent_normed, own_keys, own_values], axis=1))
    latent_halves = [half[:, :rank] for half in pack_halves]
    key_all = jnp.concatenate([half[:, rank : rank + HD] for half in pack_halves], axis=0)
    value_all = jnp.concatenate([half[:, rank + HD :] for half in pack_halves], axis=0)

    def rows_of(index):
        return slice(index * half_count, (index + 1) * half_count)

    query_halves = []
    for index in range(2):
        raw = jnp.dot(latent_halves[index], query_proj, preferred_element_type=F32)
        raw = raw.reshape(half_count, heads_local, HD)
        query_halves.append(
            rotate(
                raw, cosine[rows_of(index), None, :], sine_part[rows_of(index), None, :]
            ).astype(BF)
        )
    queries = jnp.concatenate(query_halves, axis=0)
    in_order = positions[None, :] <= positions[:, None]
    allowed = (
        row_prompt[None, :] & (jnp.logical_not(row_prompt)[:, None] | in_order)
    ) | (
        jnp.logical_not(row_prompt)[None, :]
        & jnp.logical_not(row_prompt)[:, None]
        & (row_unit[None, :] == row_unit[:, None])
        & in_order
    )

    def all_scores():
        scores = (
            jnp.einsum("qhd,kd->hqk", queries, key_all, preferred_element_type=F32) * score_scale
        )
        return jnp.where(allowed[None, :, :], scores, NEG_FILL)

    scores = all_scores()
    row_top = jnp.max(scores, axis=-1, keepdims=True)
    exp_scores = jnp.exp(scores - row_top)
    row_total = jnp.sum(exp_scores, axis=-1, keepdims=True)
    attn_probs = (exp_scores / row_total).astype(BF)
    lse = row_top + jnp.log(row_total)
    mixed = (
        jnp.einsum("hqk,kd->qhd", attn_probs, value_all, preferred_element_type=F32)
        .astype(BF)
        .reshape(plane * rows, heads_local * HD)
    )
    mixed_halves = [mixed[rows_of(0)], mixed[rows_of(1)]]
    attn_total = plane_scatter(*[contract(half, output_proj, 1, 1) for half in mixed_halves])
    hidden = inputs + attn_total

    second_inv = inv_rms(hidden)
    ffn_in = (hidden * second_inv * ffn_scale).astype(BF)
    ffn_halves = plane_gather(ffn_in)
    gate_pre = [jnp.dot(half, gate_proj, preferred_element_type=F32) for half in ffn_halves]
    up_pre = [jnp.dot(half, lift_proj, preferred_element_type=F32) for half in ffn_halves]
    activated = [
        (jax.nn.silu(gate) * lift).astype(BF) for gate, lift in zip(gate_pre, up_pre)
    ]
    ffn_total = plane_scatter(*[contract(half, drop_proj, 1, 1) for half in activated])
    block_out = hidden + ffn_total

    group_total = cont_lengths.shape[0]
    slot_total = cont_lengths.shape[1]
    pick_group = jnp.arange(group_total, dtype=jnp.int32) == g_place
    pick_slot = jnp.arange(slot_total, dtype=jnp.int32) == h_place * 2 + c_place
    own_length = jnp.sum(
        jnp.where(pick_group[:, None] & pick_slot[None, :], cont_lengths, 0)
    )
    valid_rows = jnp.logical_or(a_place == 0, within < own_length).astype(F32)
    live_count = float(group_total * prompt_total) + jnp.sum(cont_lengths).astype(F32)
    loss_scale = float(groups * plane * rows) / live_count
    target = g_flip(teacher, 1).astype(F32)
    out_grad = loss_scale * valid_rows[:, None] * (block_out - target)

    def row_product(left, right):
        return sum(contract(one, two, 0, 0) for one, two in zip(left, right)).astype(BF)

    def spread(grads):
        blocks = []
        for index in range(groups):
            pieces = []
            for grad in grads:
                size = grad.shape[0] // groups
                pieces.append(grad[index * size : (index + 1) * size])
            blocks.append(jnp.concatenate(pieces, axis=0))
        return g_scatter(blocks)

    def collected(terms, sizes, later):
        total = g_sum(terms, later)
        kept, sent = [], []
        begin = 0
        for size in sizes:
            top = total[begin : begin + size]
            low = total[begin + size : begin + 2 * size]
            begin = begin + 2 * size
            kept.append(jnp.where(is_first, top, low))
            sent.append(jnp.where(is_first, low, top))
        came = to_h(jnp.concatenate(sent, axis=0).astype(BF)).astype(F32)
        results = []
        begin = 0
        for own in kept:
            other = came[begin : begin + own.shape[0]]
            begin = begin + own.shape[0]
            results.append(
                jnp.concatenate(
                    [jnp.where(is_first, own, other), jnp.where(is_first, other, own)], axis=1
                )
            )
        return results

    out_halves = plane_gather(out_grad.astype(BF))
    drop_terms = spread([row_product(out_halves, activated)])
    grad_gate = []
    grad_lift = []
    for index in range(2):
        grad_act = jnp.dot(out_halves[index], drop_proj, preferred_element_type=F32)
        gate = gate_pre[index]
        sigmoid_gate = jax.nn.sigmoid(gate)
        grad_gate.append(
            (grad_act * up_pre[index] * sigmoid_gate * (1.0 + gate * (1.0 - sigmoid_gate))).astype(
                BF
            )
        )
        grad_lift.append((grad_act * gate * sigmoid_gate).astype(BF))

    gate_terms = spread([row_product(ffn_halves, grad_gate), row_product(ffn_halves, grad_lift)])
    grad_ffn_in = plane_scatter(
        *[
            contract(grad_gate[index], gate_proj, 1, 1)
            + contract(grad_lift[index], lift_proj, 1, 1)
            for index in range(2)
        ],
    )
    ffn_back, ffn_gain_part = norm_back(grad_ffn_in, hidden, second_inv, ffn_scale)
    grad_hidden = out_grad + ffn_back

    branch_halves = plane_gather(grad_hidden.astype(BF))
    (drop_sum,) = collected(drop_terms, [down_weight.shape[0]], branch_halves[0])
    grad_mixed = jnp.concatenate(
        [
            jnp.dot(half, output_proj, preferred_element_type=F32).astype(BF)
            for half in branch_halves
        ],
        axis=0,
    ).reshape(plane * rows, heads_local, HD)
    output_grad = row_product(branch_halves, mixed_halves)
    probs = jnp.exp(all_scores() - lse)
    grad_probs = jnp.einsum("qhd,kd->hqk", grad_mixed, value_all, preferred_element_type=F32)
    center = jnp.sum(probs * grad_probs, axis=-1, keepdims=True)
    grad_scores = (probs * (grad_probs - center)).astype(BF)
    grad_query = (
        jnp.einsum("hqk,kd->qhd", grad_scores, key_all, preferred_element_type=F32) * score_scale
    )
    key_grad = (
        jnp.einsum("hqk,qhd->kd", grad_scores, queries, preferred_element_type=F32) * score_scale
    )
    value_grad = jnp.einsum(
        "hqk,qhd->kd", probs.astype(BF), grad_mixed, preferred_element_type=F32
    )
    grad_query_raw = (
        rotate(grad_query, cosine[:, None, :], -sine_part[:, None, :])
        .reshape(plane * rows, heads_local * HD)
        .astype(BF)
    )
    raw_halves = [grad_query_raw[rows_of(0)], grad_query_raw[rows_of(1)]]
    query_up_grad = row_product(latent_halves, raw_halves)
    output_terms = spread([query_up_grad, output_grad])
    pair_total = plane_scatter(
        *[
            jnp.concatenate(
                [
                    contract(raw_halves[index], query_proj, 1, 1),
                    key_grad[rows_of(index)],
                    value_grad[rows_of(index)],
                ],
                axis=1,
            )
            for index in range(2)
        ],
    )
    gate_sum, lift_sum = collected(
        gate_terms, [gate_weight.shape[0], up_weight.shape[0]], pair_total
    )
    latent_back, query_gain_part = norm_back(
        pair_total[:, :rank], latent, latent_inv, latent_scale
    )
    grad_key_raw = rotate(pair_total[:, rank : rank + HD], own_cosine, -own_sine)
    grad_pack = jnp.concatenate(
        [g_flip(latent_back, 1), grad_key_raw, pair_total[:, rank + HD :]], axis=1
    ).astype(BF)
    gain_rows = jnp.concatenate([query_gain_part, ffn_gain_part]).reshape(2, pack_cols)
    padded = rows + 16
    grad_pack = jnp.concatenate(
        [grad_pack, jnp.pad(gain_rows, ((0, 14), (0, 0))).astype(BF)], axis=0
    )
    pack_grads = plane_gather(grad_pack)
    query_up_sum, output_sum = collected(
        output_terms, [query_up.shape[0], out_weight.shape[0]], pack_grads[0]
    )
    wide_normed = [
        jnp.pad(half, ((0, 0), (0, 16), (0, 0))).reshape(4 * padded, slice_rows)
        for half in (normed_near, normed_far)
    ]
    shared_grad = sum(contract(one, two, 0, 0) for one, two in zip(wide_normed, pack_grads))
    slice_grads = [contract(half, shared_proj, 1, 1) for half in pack_grads]
    attn_gain_slice = sum(
        jnp.sum(grad * value.astype(F32), axis=0)
        for grad, value in zip(slice_grads, wide_normed)
    ) / shared_slice[:, pack_cols].astype(F32)
    gain_totals = sum(
        jnp.sum(half.reshape(4, padded, pack_cols)[:, rows : rows + 2].astype(F32), axis=0)
        for half in pack_grads
    ).reshape(rank + width)
    place = h_place * 4 + a_place * 2 + c_place
    query_gain_slice = lax.dynamic_index_in_dim(
        gain_totals[:rank].reshape(groups, plane, q_rows), place, 1, keepdims=False
    )
    query_gain_slice = jnp.pad(query_gain_slice, ((0, 0), (0, w_rows - q_rows)))
    ffn_gain_slice = lax.dynamic_index_in_dim(
        gain_totals[rank:].reshape(groups, plane, w_rows), place, 1, keepdims=False
    )
    gain_grad_cols = jnp.stack(
        [attn_gain_slice, ffn_gain_slice.reshape(slice_rows), query_gain_slice.reshape(slice_rows)],
        axis=1,
    )
    shared_out = jnp.concatenate(
        [shared_grad, jnp.pad(gain_grad_cols, ((0, 0), (0, 125)))], axis=1
    ).astype(BF)
    shared_terms = g_scatter(
        [shared_out[index * w_rows : (index + 1) * w_rows] for index in range(groups)]
    )

    near_grad, far_grad = [
        grad.reshape(4, padded, slice_rows)[:, :rows].astype(BF) for grad in slice_grads
    ]
    back_a = to_a(jnp.stack([near_grad[1], far_grad[1]]))
    back_h = to_h(jnp.stack([near_grad[2], far_grad[2]]))
    back_ha = to_ha(jnp.stack([near_grad[3], far_grad[3]]))
    mine = jnp.stack([near_grad[0], back_a[0], back_h[0], back_ha[0]])
    others = to_c(jnp.stack([far_grad[0], back_a[1], back_h[1], back_ha[1]]))
    grad_normed = plane_back(
        jnp.stack([mine, others]).reshape(2, 2, 2, rows, slice_rows)
    ).reshape(plane, rows, groups, w_rows)
    grad_normed = grad_normed.transpose(1, 2, 0, 3).reshape(rows, width).astype(F32)
    first_back, _ = norm_back(grad_normed, inputs, first_inv, attn_scale)
    input_grad = grad_hidden + first_back
    shared_sum = sum(term.astype(F32) for term in shared_terms)

    return (
        g_flip(block_out, 1),
        g_flip(input_grad, 1),
        shared_sum[:, :rank],
        shared_sum[:, rank : rank + HD],
        shared_sum[:, rank + HD : pack_cols],
        shared_sum[:, pack_cols],
        shared_sum[:, pack_cols + 1],
        shared_sum[:q_rows, pack_cols + 2],
        query_up_sum,
        output_sum,
        gate_sum,
        lift_sum,
        drop_sum,
    )


def solution(mesh):
    dp, tensor = mesh.shape["dp"], mesh.shape["tensor"]
    fine = Mesh(mesh.devices.reshape(dp // 2, 2, tensor // 2, 2), ("g", "h", "a", "c"))
    rows = P(("g", "h", "a", "c"), None)
    vector = P(("g", "h", "a", "c"))
    block = P(("g", "h"), ("a", "c"))
    return jax.shard_map(
        layer,
        mesh=fine,
        in_specs=(rows, rows, P()) + (rows,) * 3 + (vector,) * 3 + (block,) * 5,
        out_specs=(rows,) * 5 + (vector,) * 3 + (block,) * 5,
        check_vma=False,
    )
```
